32 devices in a mesh: groups: 2 (over y), blk: 4 (over z), head: 2 (over x), rep: 2 (over core).
Axes of the slice: x: 2, y: 2, z: 4, core: 2. Of those that a mesh axis runs over, the one named last changes fastest.
Arguments:
- query: bfloat16 [128, 16384], P(('groups', 'blk', 'rep'), 'head'), parts along dimension 0, may hold values from -200 to 200
- keys: bfloat16 [8, 2, 2048, 8, 128], P(('groups', 'blk'), 'rep', None, 'head'), parts along dimension 0, may hold values from -8 to 8
- values: bfloat16 [8, 2, 2048, 8, 128], P(('groups', 'blk'), 'rep', None, 'head'), parts along dimension 0, may hold values from -6 to 6
- lengths: int32 [128], P('groups'), parts along dimension 0, may hold values from 2 to 8192, as said below
- out_weight: bfloat16 [16384, 16384], P('head', ('blk', 'rep')), may hold values from -0.046875 to 0.046875
Outputs:
- projected: bfloat16 [128, 16384], P(('groups', 'head'), ('blk', 'rep')), parts along dimension 0
The draws below stay inside these ranges and needn't reach their ends.
There are 2 independent parts, one for each index of `groups`. The reference program is written for one: setup_inputs(seed, part) draws one part's arguments, and reference() takes and returns one part's arrays. A program takes and returns all parts, laid end to end along the dimension named above; an argument that names none is the same for every part. Nothing has to cross between parts.
Inputs may be any that keep to these rules, and one draw needn't show every extreme that they name: `lengths`: some request of every draw sees all 8192 positions.
All inputs are finite; a program needn't handle non-finite values.
Results may differ from the reference program's by a relative error of at most 0.012.
Values may be sent and summed in bfloat16 or wider, within the bound.
A program may use at most 128 MiB of HBM per device.

```python
import jax
import jax.numpy as jnp
from jax import lax

D = 16384
HQ = 128
KVH = 8
HD = 128
ROWS_DEV = 8
SLAB = 2048
SPAN = 4
STRIDE = 1
QPK = 16
REQ = 64
N_BLK = 4
N_REP = 2


def joint_draw(key):
    base = jax.random.fold_in(key, 11)
    key_cache, key_query = jax.random.split(base, 2)
    cache_shape = (N_BLK, N_REP, SLAB, KVH, HD)
    cached = jnp.clip(jax.random.normal(key_cache, cache_shape, jnp.float32), -6.0, 6.0)
    queries = jnp.clip(jax.random.normal(key_query, (REQ, HQ * HD), jnp.float32), -6.0, 6.0)
    return (queries, cached)


def draw_query(key, part):
    return joint_draw(key)[0].astype(jnp.bfloat16)


def draw_keys(key, part):
    return joint_draw(key)[1].astype(jnp.bfloat16)


def draw_lengths(key, part):
    base = jax.random.fold_in(key, 23)
    key_len, key_full = jax.random.split(base, 2)
    longest_len = SPAN * SLAB
    drawn = jax.random.randint(key_len, (REQ,), 2, longest_len + 1)
    chosen = jax.random.randint(key_full, (), 0, REQ)
    drawn = drawn.at[chosen].set(longest_len)
    return drawn.astype(jnp.int32)


def levels(key, extent, cuts, low, top_value):
    gain = 1.0
    for axis_at, shards_of in cuts:
        heights = jax.random.uniform(jax.random.fold_in(jax.random.fold_in(key, 6), axis_at), (shards_of,), jnp.float32, low / len(cuts), top_value / len(cuts))
        gain = gain * jnp.repeat(jnp.exp(heights), extent[axis_at] // shards_of).reshape((-1,) + (1,) * (len(extent) - 1 - axis_at))
    return gain


def gaussian(own_key, extent, scale, most, cuts=(), held_as=jnp.bfloat16):
    array = jax.random.normal(own_key, extent, jnp.float32) * scale
    if len(cuts) > 0:
        array = levels(own_key, extent, cuts, -0.22, 0.18) * array
    return jnp.clip(array, min=-most, max=most).astype(held_as)


def setup_inputs(seed: int = 0, part: int = 0) -> dict:
    key_of = jax.random.split(jax.random.key(seed), 6)
    part_splits = jax.random.split(jax.random.fold_in(key_of[5], part), 6)
    query = draw_query(jax.random.fold_in(jax.random.fold_in(key_of[5], part), 71), part)
    keys = draw_keys(jax.random.fold_in(jax.random.fold_in(key_of[5], part), 71), part)
    values = gaussian(part_splits[2], (N_BLK, N_REP, SLAB, KVH, HD), 1.0, 6.0, ((0, 4), (1, 2), (3, 2)))
    lengths = draw_lengths(jax.random.fold_in(jax.random.fold_in(key_of[5], part), 71), part)
    out_weight = gaussian(key_of[4], (HQ * HD, D), (HQ * HD) ** -0.5, 0.046875, ((0, 2), (1, 8)))
    return dict(query=query, keys=keys, values=values, lengths=lengths, out_weight=out_weight)


NEG = -1e30


def reference(query, keys, values, lengths, out_weight):
    key_docs = keys.reshape(SPAN, STRIDE, N_REP, SLAB, KVH, HD)
    value_docs = values.reshape(SPAN, STRIDE, N_REP, SLAB, KVH, HD)
    query_rows = query.reshape(N_BLK * N_REP, ROWS_DEV, HQ * HD)
    length_rows = lengths.reshape(N_BLK * N_REP, ROWS_DEV)
    pair_ids = jnp.arange(N_BLK * N_REP, dtype=jnp.int32)

    def owner_attention(pieces):
        pair_id, query_block, length_block = pieces
        document = (pair_id // N_REP) % STRIDE
        rep_index = pair_id % N_REP
        key_block = key_docs[:, document, rep_index]
        value_block = value_docs[:, document, rep_index]
        queries = query_block.astype(jnp.float32).reshape(ROWS_DEV, KVH, QPK, HD)
        scores = jnp.einsum("rkgd,sjkd->rkgsj", queries, key_block.astype(jnp.float32)) * (HD ** -0.5)
        positions = jnp.arange(SPAN, dtype=jnp.int32)[:, None] * SLAB + jnp.arange(SLAB, dtype=jnp.int32)[None, :]
        live_mask = positions[None, :, :] < length_block[:, None, None]
        live_mask = live_mask[:, None, None]
        best_score = jnp.max(jnp.where(live_mask, scores, NEG), axis=-1)
        weights = jnp.where(live_mask, jnp.exp(scores - best_score[..., None]), 0.0)
        block_sum = jnp.sum(weights, axis=-1)
        rounded = lax.optimization_barrier(weights.astype(jnp.bfloat16))
        partial_value = jnp.einsum("rkgsj,sjkd->rkgsd", rounded.astype(jnp.float32), value_block.astype(jnp.float32))
        partial_value = lax.optimization_barrier(partial_value.astype(jnp.bfloat16)).astype(jnp.float32)
        overall = jnp.max(best_score, axis=-1)
        factors = jnp.exp(best_score - overall[..., None])
        summed = jnp.sum(factors * block_sum, axis=-1)
        merged = jnp.sum(factors[..., None] * partial_value, axis=3)
        attended = (merged / summed[..., None]).astype(jnp.bfloat16)
        return attended.reshape(ROWS_DEV, HQ * HD)

    attended = lax.map(owner_attention, (pair_ids, query_rows, length_rows))
    attended = attended.reshape(REQ, HQ * HD)
    return jnp.dot(attended, out_weight, preferred_element_type=jnp.float32).astype(jnp.bfloat16)
```

```python
import functools
import jax
import jax.numpy as jnp
from jax import lax
from jax.experimental import pallas as pl
from jax.experimental.pallas import tpu as pltpu
from jax.sharding import PartitionSpec as P

NEG = -1e30
LOG2E = 1.4426950408889634
MESH = pl.DeviceIdType.MESH


def remote(src, dst, ssem, rsem, where):
    return pltpu.make_async_remote_copy(
        src_ref=src, dst_ref=dst, send_sem=ssem, recv_sem=rsem,
        device_id=where, device_id_type=MESH)


def kernel(
    dims, lengths, query, keys, values, weight, out,
    wv, kraw, vraw, kh, vt, fbuf, sbuf, wbuf, qbuf, qmat, pbuf, pstat, rbuf, rstat,
    abuf, acc, hsend, hrecv,
    wsem, ksem, q_ss, q_rs, p_ss, p_rs, t_ss, t_rs, a_ss, a_rs, c_ss, c_rs, h_ss, h_rs,
):
    B, R, H, S, stride, rows, K, G, HD, slab = dims
    heads = pl.ds
    group = G * rows
    lanes = S * group
    feat = G * HD
    cols = weight.shape[1]
    total = B * R * rows
    share = total // H
    nc = hsend.shape[1]
    cw = cols // nc
    scale2 = (HD ** -0.5) * LOG2E
    me_b = lax.axis_index("blk")
    me_r = lax.axis_index("rep")
    me_h = lax.axis_index("head")
    p = me_b // stride
    base = lax.rem(me_b, stride)

    def holder(q):
        return {"blk": q * stride + base}

    kcopy = pltpu.make_async_copy(keys, kraw, ksem.at[0])
    vcopy = pltpu.make_async_copy(values, vraw, ksem.at[1])
    kcopy.start()
    vcopy.start()
    wcopies = [
        pltpu.make_async_copy(weight.at[pl.ds(k * feat, feat)], wv.at[pl.ds(k * feat, feat)], wsem.at[k])
        for k in range(K)
    ]
    for c in wcopies:
        c.start()

    barrier = pltpu.get_barrier_semaphore()
    for d in range(1, S):
        pl.semaphore_signal(barrier, inc=1, device_id=holder(lax.rem(p + d, S)), device_id_type=MESH)
    for d in range(1, R):
        pl.semaphore_signal(barrier, inc=1, device_id={"rep": lax.rem(me_r + d, R)}, device_id_type=MESH)
    for d in range(1, H):
        pl.semaphore_signal(barrier, inc=1, device_id={"head": lax.rem(me_h + d, H)}, device_id_type=MESH)
    if stride > 1:
        for d in (1, B - 1):
            pl.semaphore_signal(barrier, inc=1, device_id={"blk": lax.rem(me_b + d, B)}, device_id_type=MESH)
    pl.semaphore_wait(barrier, (S - 1) + (R - 1) + (H - 1) + (2 if stride > 1 else 0))

    def q_move(k, o, side, src):
        to = p + 1 if side == 0 else p - 1
        return remote(src, qbuf.at[k, o], q_ss.at[k, o, side], q_rs.at[k, o], holder(to))

    def own_q(k):
        return query.at[:, pl.ds(k * feat, feat)]

    def q_start(k):
        @pl.when(p < S - 1)
        def _():
            q_move(k, p, 0, own_q(k)).start()

        @pl.when(p > 0)
        def _():
            q_move(k, p, 1, own_q(k)).start()

        qbuf[k, p] = query[:, k * feat:(k + 1) * feat]

    def q_hop(k, h):
        @pl.when(p >= h)
        def _():
            o = p - h
            q_move(k, o, 0, qbuf.at[k, o]).wait_recv()

            @pl.when(p < S - 1)
            def _():
                q_move(k, o, 0, qbuf.at[k, o]).start()

        @pl.when(p + h < S)
        def _():
            o = p + h
            q_move(k, o, 1, qbuf.at[k, o]).wait_recv()

            @pl.when(p > 0)
            def _():
                q_move(k, o, 1, qbuf.at[k, o]).start()

    def q_tick(t):
        if t < K:
            q_start(t)
        for h in range(S - 1, 0, -1):
            if 0 <= t - h < K:
                q_hop(t - h, h)

    def q_drain():
        for k in range(K):
            @pl.when(p < S - 1)
            def _():
                q_move(k, p, 0, own_q(k)).wait_send()
                for h in range(1, S):
                    @pl.when(p >= h)
                    def _():
                        q_move(k, p - h, 0, qbuf.at[k, p - h]).wait_send()

            @pl.when(p > 0)
            def _():
                q_move(k, p, 1, own_q(k)).wait_send()
                for h in range(1, S):
                    @pl.when(p + h < S)
                    def _():
                        q_move(k, p + h, 1, qbuf.at[k, p + h]).wait_send()

    sub = lax.rem(lax.broadcasted_iota(jnp.int32, (1, group), 1), rows)
    pieces = []
    for o in range(S):
        first = ((o * stride + base) * R + me_r) * rows
        piece = jnp.zeros((1, group), jnp.int32)
        for r in range(rows):
            piece = jnp.where(sub == r, lengths[first + r], piece)
        pieces.append(piece)
    live_to = jnp.concatenate(pieces, axis=1) - p * slab

    step = 256

    def split(c, carry):
        src = pl.ds(pl.multiple_of(c * step * K, step * K), step * K)
        dst = pl.ds(pl.multiple_of(c * step, step), step)
        fbuf[0] = kraw[src, :].astype(jnp.float32)
        fbuf[1] = vraw[src, :].astype(jnp.float32)
        for k in range(K):
            kh[k, dst, :] = fbuf[0, pl.ds(k, step, stride=K), :].astype(jnp.bfloat16)
            vt[k, :, dst] = fbuf[1, pl.ds(k, step, stride=K), :].T.astype(jnp.bfloat16)
        return carry

    def attend(k):
        for o in range(S):
            x = qbuf[k, o].astype(jnp.float32)
            x = jnp.concatenate([x[:, g * HD:(g + 1) * HD] for g in range(G)], axis=0)
            qmat[o * group:(o + 1) * group, :] = x.astype(jnp.bfloat16)
        qk = qmat[...]
        iota = lax.broadcasted_iota(jnp.int32, (step, lanes), 0)

        def first(c, m):
            at = pl.ds(pl.multiple_of(c * step, step), step)
            s = lax.dot_general(kh[k, at, :], qk, (((1,), (1,)), ((), ())), preferred_element_type=jnp.float32)
            s = jnp.where(iota < live_to - c * step, s, NEG)
            sbuf[at, :] = s
            return jnp.maximum(m, jnp.max(s.reshape(step // 8, 8, lanes), axis=0))

        m = lax.fori_loop(0, slab // step, first, jnp.full((8, lanes), NEG, jnp.float32))
        m = jnp.max(m, axis=0, keepdims=True)

        def second(c, l):
            at = pl.ds(pl.multiple_of(c * step, step), step)
            e = jnp.exp2((sbuf[at, :] - m) * scale2)
            wbuf[at, :] = e.astype(jnp.bfloat16)
            return l + jnp.sum(e.reshape(step // 8, 8, lanes), axis=0)

        l = lax.fori_loop(0, slab // step, second, jnp.zeros((8, lanes), jnp.float32))
        l = jnp.sum(l, axis=0, keepdims=True)
        part = jnp.dot(vt[k], wbuf[...], preferred_element_type=jnp.float32).astype(jnp.bfloat16)
        four = jnp.zeros((4, group), jnp.float32)
        for o in range(S):
            at = slice(o * group, (o + 1) * group)
            pbuf[k, o] = part[:, at]
            pstat[k, o, 0:1] = m[:, at]
            pstat[k, o, 1:2] = l[:, at]

    def p_move(k, to, frm):
        return (
            remote(pbuf.at[k, to], rbuf.at[k, frm], p_ss.at[k, to], p_rs.at[k, frm], holder(to)),
            remote(pstat.at[k, to], rstat.at[k, frm], t_ss.at[k, to], t_rs.at[k, frm], holder(to)),
        )

    def p_send(k):
        for d in range(1, S):
            for c in p_move(k, lax.rem(p + d, S), p):
                c.start()
        rbuf[k, p] = pbuf[k, p]
        rstat[k, p] = pstat[k, p]

    def a_line(k, o, side):
        to = me_b + 1 if side == 0 else me_b - 1
        slot = abuf.at[k, o * R + me_r]
        return remote(slot, slot, a_ss.at[k, o, side], a_rs.at[k, o], {"blk": to})

    def a_core(k, o, d):
        slot = abuf.at[k, o * R + me_r]
        return remote(slot, slot, c_ss.at[k, o, d - 1], c_rs.at[k, o, d - 1], {"rep": lax.rem(me_r + d, R)})

    def a_core_in(k, o, d):
        slot = abuf.at[k, o * R + lax.rem(me_r + R - d, R)]
        return remote(slot, slot, c_ss.at[k, o, d - 1], c_rs.at[k, o, d - 1], {"rep": lax.rem(me_r + d, R)})

    def combine(k):
        for d in range(1, S):
            for c in p_move(k, lax.rem(p + d, S), lax.rem(p + S - d, S)):
                c.wait_recv()
        best = [rstat[k, s, 0:1] for s in range(S)]
        top = functools.reduce(jnp.maximum, best)
        den = jnp.zeros((1, group), jnp.float32)
        num = jnp.zeros((HD, group), jnp.float32)
        for s in range(S):
            f = jnp.exp2((best[s] - top) * scale2)
            den = den + f * rstat[k, s, 1:2]
            num = num + f * rbuf[k, s].astype(jnp.float32)
        att = (num / den).T
        att = jnp.concatenate([att[g * rows:(g + 1) * rows, :] for g in range(G)], axis=1)
        abuf[k, me_b * R + me_r] = att.astype(jnp.bfloat16)

        @pl.when(me_b < B - 1)
        def _():
            a_line(k, me_b, 0).start()

        @pl.when(me_b > 0)
        def _():
            a_line(k, me_b, 1).start()

        for d in range(1, R):
            a_core(k, me_b, d).start()

    def a_hop(k, h):
        @pl.when(me_b >= h)
        def _():
            o = me_b - h
            a_line(k, o, 0).wait_recv()

            @pl.when(me_b < B - 1)
            def _():
                a_line(k, o, 0).start()

            for d in range(1, R):
                a_core(k, o, d).start()

        @pl.when(me_b + h < B)
        def _():
            o = me_b + h
            a_line(k, o, 1).wait_recv()

            @pl.when(me_b > 0)
            def _():
                a_line(k, o, 1).start()

            for d in range(1, R):
                a_core(k, o, d).start()

    def a_drain():
        for k in range(K):
            for o in range(B):
                for d in range(1, R):
                    a_core(k, o, d).wait_send()

            @pl.when(me_b < B - 1)
            def _():
                for o in range(B):
                    @pl.when(me_b >= o)
                    def _():
                        a_line(k, o, 0).wait_send()

            @pl.when(me_b > 0)
            def _():
                for o in range(B):
                    @pl.when(me_b <= o)
                    def _():
                        a_line(k, o, 1).wait_send()

    def h_move(n, d):
        return remote(hsend.at[d - 1, n], hrecv.at[d - 1, n], h_ss.at[d - 1, n], h_rs.at[d - 1, n],
                      {"head": lax.rem(me_h + d, H)})

    def project(k):
        wcopies[k].wait()
        for o in range(B):
            for d in range(1, R):
                a_core_in(k, o, d).wait_recv()
        rowsk = jnp.concatenate([abuf[k, i].astype(jnp.float32) for i in range(B * R)], axis=0).astype(jnp.bfloat16)
        for n in range(nc):
            w = wv[k * feat:(k + 1) * feat, n * cw:(n + 1) * cw]
            y = jnp.dot(rowsk, w, preferred_element_type=jnp.float32)
            if k > 0:
                y = y + acc[n]
            acc[n] = y
            if k == K - 1:
                for d in range(1, H):
                    to = lax.rem(me_h + d, H)
                    hsend[d - 1, n] = acc[n, pl.ds(pl.multiple_of(to * share, share), share), :].astype(jnp.bfloat16)
                    h_move(n, d).start()

    q_tick(0)
    kcopy.wait()
    vcopy.wait()
    lax.fori_loop(0, slab // step, split, 0)
    for t in range(1, S):
        q_tick(t)
    done_hops = []
    todo = []

    for k in range(K):
        attend(k)
        p_send(k)
        if k + 1 < K:
            q_tick(S + k)
        if k >= 2:
            a_hop(k - 2, 1)
        if k >= 1:
            combine(k - 1)
        if k >= 3:
            for h in range(2, B):
                a_hop(k - 3, h)
            project(k - 3)
    combine(K - 1)
    left = list(range(max(0, K - 3), K))
    for k in left:
        if k > K - 3 or K < 3:
            a_hop(k, 1)
    for k in left:
        for h in range(2, B):
            a_hop(k, h)
        project(k)
    own = pl.ds(pl.multiple_of(me_h * share, share), share)
    for n in range(nc):
        y = acc[n, own, :]
        for d in range(1, H):
            h_move(n, d).wait_recv()
            y = y + hrecv[d - 1, n].astype(jnp.float32)
        out[:, n * cw:(n + 1) * cw] = y.astype(jnp.bfloat16)
    q_drain()
    for k in range(K):
        for d in range(1, S):
            for c in p_move(k, lax.rem(p + d, S), p):
                c.wait_send()
    a_drain()
    for n in range(nc):
        for d in range(1, H):
            h_move(n, d).wait_send()


def body(query, keys, values, lengths, out_weight):
    rows = query.shape[0]
    slab, K, HD = keys.shape[2:]
    B = lax.axis_size("blk")
    R = lax.axis_size("rep")
    H = lax.axis_size("head")
    S = min(8, B)
    stride = B // S
    G = query.shape[1] // (K * HD)
    feat = G * HD
    group = G * rows
    lanes = S * group
    depth, cols = out_weight.shape
    total = B * R * rows
    share = total // H
    nc = max(1, cols // 512)
    cw = cols // nc
    dims = (B, R, H, S, stride, rows, K, G, HD, slab)
    bf, f32 = jnp.bfloat16, jnp.float32
    vm, dma = pltpu.VMEM, pltpu.SemaphoreType.DMA
    any_spec = pl.BlockSpec(memory_space=pltpu.HBM)
    return pl.pallas_call(
        functools.partial(kernel, dims),
        out_shape=jax.ShapeDtypeStruct((share, cols), bf),
        in_specs=[
            pl.BlockSpec(memory_space=pltpu.SMEM),
            pl.BlockSpec(memory_space=pltpu.VMEM),
            any_spec, any_spec, any_spec,
        ],
        out_specs=pl.BlockSpec(memory_space=pltpu.VMEM),
        scratch_shapes=[
            vm((depth, cols), bf),
            vm((slab * K, HD), bf),
            vm((slab * K, HD), bf),
            vm((K, slab, HD), bf),
            vm((K, HD, slab), bf),
            vm((2, 256 * K, HD), f32),
            vm((slab, lanes), f32),
            vm((slab, lanes), bf),
            vm((K, S, rows, feat), bf),
            vm((lanes, HD), bf),
            vm((K, S, HD, group), bf),
            vm((K, S, 8, group), f32),
            vm((K, S, HD, group), bf),
            vm((K, S, 8, group), f32),
            vm((K, B * R, rows, feat), bf),
            vm((nc, total, cw), f32),
            vm((max(1, H - 1), nc, share, cw), bf),
            vm((max(1, H - 1), nc, share, cw), bf),
            dma((K,)),
            dma((2,)),
            dma((K, S, 2)), dma((K, S)),
            dma((K, S)), dma((K, S)),
            dma((K, S)), dma((K, S)),
            dma((K, B, 2)), dma((K, B)),
            dma((K, B, max(1, R - 1))), dma((K, B, max(1, R - 1))),
            dma((max(1, H - 1), nc)), dma((max(1, H - 1), nc)),
        ],
        compiler_params=pltpu.CompilerParams(
            collective_id=0, has_side_effects=True, vmem_limit_bytes=61 * 1024 * 1024),
        name="attend_project",
    )(lengths, query, keys.reshape(slab * K, HD), values.reshape(slab * K, HD), out_weight)


def solution(mesh):
    return jax.shard_map(
        body,
        mesh=mesh,
        in_specs=(
            P(("groups", "blk", "rep"), "head"),
            P(("groups", "blk"), "rep", None, "head", None),
            P(("groups", "blk"), "rep", None, "head", None),
            P("groups"),
            P("head", ("blk", "rep")),
        ),
        out_specs=P(("groups", "head"), ("blk", "rep")),
        check_vma=False,
    )
```

```python
import functools
import jax
import jax.numpy as jnp
from jax import lax
from jax.experimental import pallas as pl
from jax.experimental.pallas import tpu as pltpu
from jax.sharding import PartitionSpec as P

NEG = -1e30
LOG2E = 1.4426950408889634
MESH = pl.DeviceIdType.MESH


def remote(src, dst, ssem, rsem, where):
    return pltpu.make_async_remote_copy(
        src_ref=src, dst_ref=dst, send_sem=ssem, recv_sem=rsem,
        device_id=where, device_id_type=MESH)


def kernel(
    dims, lengths, query, keys, values, weight, out,
    wv, kraw, vraw, kh, vt, fbuf, sbuf, wbuf, qbuf, qmat, pbuf, pstat, rbuf, rstat,
    abuf, acc, hsend, hrecv, lin, lstat, lout, lostat,
    wsem, ksem, q_ss, q_rs, p_ss, p_rs, t_ss, t_rs, a_ss, a_rs, c_ss, c_rs, h_ss, h_rs,
    l_ss, l_rs, s_ss, s_rs,
):
    B, R, H, S, stride, rows, K, G, HD, slab = dims
    heads = pl.ds
    group = G * rows
    lanes = S * group
    feat = G * HD
    cols = weight.shape[1]
    total = B * R * rows
    share = total // H
    nc = hsend.shape[1]
    cw = cols // nc
    scale2 = (HD ** -0.5) * LOG2E
    me_b = lax.axis_index("blk")
    me_r = lax.axis_index("rep")
    me_h = lax.axis_index("head")
    p = me_b // stride
    base = lax.rem(me_b, stride)

    def holder(q):
        return {"blk": q * stride + base}

    kcopy = pltpu.make_async_copy(keys, kraw, ksem.at[0])
    vcopy = pltpu.make_async_copy(values, vraw, ksem.at[1])
    kcopy.start()
    vcopy.start()
    wcopies = [
        pltpu.make_async_copy(weight.at[pl.ds(k * feat, feat)], wv.at[pl.ds(k * feat, feat)], wsem.at[k])
        for k in range(K)
    ]

    barrier = pltpu.get_barrier_semaphore()
    for d in range(1, S):
        pl.semaphore_signal(barrier, inc=1, device_id=holder(lax.rem(p + d, S)), device_id_type=MESH)
    for d in range(1, R):
        pl.semaphore_signal(barrier, inc=1, device_id={"rep": lax.rem(me_r + d, R)}, device_id_type=MESH)
    for d in range(1, H):
        pl.semaphore_signal(barrier, inc=1, device_id={"head": lax.rem(me_h + d, H)}, device_id_type=MESH)
    if stride > 1:
        for d in (1, B - 1):
            pl.semaphore_signal(barrier, inc=1, device_id={"blk": lax.rem(me_b + d, B)}, device_id_type=MESH)
    pl.semaphore_wait(barrier, (S - 1) + (R - 1) + (H - 1) + (2 if stride > 1 else 0))

    def q_move(k, o, side, src):
        to = p + 1 if side == 0 else p - 1
        return remote(src, qbuf.at[k, o], q_ss.at[k, o, side], q_rs.at[k, o], holder(to))

    def own_q(k):
        return query.at[:, pl.ds(k * feat, feat)]

    def q_start(k):
        @pl.when(p < S - 1)
        def _():
            q_move(k, p, 0, own_q(k)).start()

        @pl.when(p > 0)
        def _():
            q_move(k, p, 1, own_q(k)).start()

        qbuf[k, p] = query[:, k * feat:(k + 1) * feat]

    def q_hop(k, h):
        @pl.when(p >= h)
        def _():
            o = p - h
            q_move(k, o, 0, qbuf.at[k, o]).wait_recv()

            @pl.when(p < S - 1)
            def _():
                q_move(k, o, 0, qbuf.at[k, o]).start()

        @pl.when(p + h < S)
        def _():
            o = p + h
            q_move(k, o, 1, qbuf.at[k, o]).wait_recv()

            @pl.when(p > 0)
            def _():
                q_move(k, o, 1, qbuf.at[k, o]).start()

    hops = sorted((k + 2 * h, h, k) for k in range(K) for h in range(1, S))

    def q_ready(k):
        while hops and hops[0][0] <= k + 2 * (S - 1):
            _, h, j = hops.pop(0)
            q_hop(j, h)

    def q_drain():
        for k in range(K):
            @pl.when(p < S - 1)
            def _():
                q_move(k, p, 0, own_q(k)).wait_send()
                for h in range(1, S):
                    @pl.when(p >= h)
                    def _():
                        q_move(k, p - h, 0, qbuf.at[k, p - h]).wait_send()

            @pl.when(p > 0)
            def _():
                q_move(k, p, 1, own_q(k)).wait_send()
                for h in range(1, S):
                    @pl.when(p + h < S)
                    def _():
                        q_move(k, p + h, 1, qbuf.at[k, p + h]).wait_send()

    sub = lax.rem(lax.broadcasted_iota(jnp.int32, (1, group), 1), rows)
    pieces = []
    for o in range(S):
        first = ((o * stride + base) * R + me_r) * rows
        piece = jnp.zeros((1, group), jnp.int32)
        for r in range(rows):
            piece = jnp.where(sub == r, lengths[first + r], piece)
        pieces.append(piece)
    live_to = jnp.concatenate(pieces, axis=1) - p * slab

    step = 256

    def split(c, carry):
        src = pl.ds(pl.multiple_of(c * step * K, step * K), step * K)
        dst = pl.ds(pl.multiple_of(c * step, step), step)
        fbuf[0] = kraw[src, :].astype(jnp.float32)
        fbuf[1] = vraw[src, :].astype(jnp.float32)
        for k in range(K):
            kh[k, dst, :] = fbuf[0, pl.ds(k, step, stride=K), :].astype(jnp.bfloat16)
            vt[k, :, dst] = fbuf[1, pl.ds(k, step, stride=K), :].T.astype(jnp.bfloat16)
        return carry

    def attend(k):
        for o in range(S):
            x = qbuf[k, o].astype(jnp.float32)
            x = jnp.concatenate([x[:, g * HD:(g + 1) * HD] for g in range(G)], axis=0)
            qmat[o * group:(o + 1) * group, :] = x.astype(jnp.bfloat16)
        qk = qmat[...]
        iota = lax.broadcasted_iota(jnp.int32, (step, lanes), 0)

        def first(c, m):
            at = pl.ds(pl.multiple_of(c * step, step), step)
            s = lax.dot_general(kh[k, at, :], qk, (((1,), (1,)), ((), ())), preferred_element_type=jnp.float32)
            s = jnp.where(iota < live_to - c * step, s, NEG)
            sbuf[at, :] = s
            return jnp.maximum(m, jnp.max(s.reshape(step // 8, 8, lanes), axis=0))

        m = lax.fori_loop(0, slab // step, first, jnp.full((8, lanes), NEG, jnp.float32), unroll=2)
        m = jnp.max(m, axis=0, keepdims=True)

        def second(c, l):
            at = pl.ds(pl.multiple_of(c * step, step), step)
            e = jnp.exp2((sbuf[at, :] - m) * scale2)
            wbuf[at, :] = e.astype(jnp.bfloat16)
            return l + jnp.sum(e.reshape(step // 8, 8, lanes), axis=0)

        l = lax.fori_loop(0, slab // step, second, jnp.zeros((8, lanes), jnp.float32), unroll=2)
        l = jnp.sum(l, axis=0, keepdims=True)
        part = jnp.dot(vt[k], wbuf[...], preferred_element_type=jnp.float32).astype(jnp.bfloat16)
        for o in range(S):
            at = slice(o * group, (o + 1) * group)
            pbuf[k, o] = part[:, at]
            pstat[k, o, 0:1] = m[:, at]
            pstat[k, o, 1:2] = l[:, at]

    def p_move(k, to, frm):
        return (
            remote(pbuf.at[k, to], rbuf.at[k, frm], p_ss.at[k, to], p_rs.at[k, frm], holder(to)),
            remote(pstat.at[k, to], rstat.at[k, frm], t_ss.at[k, to], t_rs.at[k, frm], holder(to)),
        )

    def p_send(k):
        for d in range(1, S):
            for c in p_move(k, lax.rem(p + d, S), p):
                c.start()
        rbuf[k, p] = pbuf[k, p]
        rstat[k, p] = pstat[k, p]

    def a_line(k, o, side):
        to = me_b + 1 if side == 0 else me_b - 1
        slot = abuf.at[k, o * R + me_r]
        return remote(slot, slot, a_ss.at[k, o, side], a_rs.at[k, o], {"blk": to})

    def a_core(k, o, d):
        slot = abuf.at[k, o * R + me_r]
        return remote(slot, slot, c_ss.at[k, o, d - 1], c_rs.at[k, o, d - 1], {"rep": lax.rem(me_r + d, R)})

    def a_core_in(k, o, d):
        slot = abuf.at[k, o * R + lax.rem(me_r + R - d, R)]
        return remote(slot, slot, c_ss.at[k, o, d - 1], c_rs.at[k, o, d - 1], {"rep": lax.rem(me_r + d, R)})

    def combine(k):
        for d in range(1, S):
            for c in p_move(k, lax.rem(p + d, S), lax.rem(p + S - d, S)):
                c.wait_recv()
        best = [rstat[k, s, 0:1] for s in range(S)]
        top = functools.reduce(jnp.maximum, best)
        den = jnp.zeros((1, group), jnp.float32)
        num = jnp.zeros((HD, group), jnp.float32)
        for s in range(S):
            f = jnp.exp2((best[s] - top) * scale2)
            den = den + f * rstat[k, s, 1:2]
            num = num + f * rbuf[k, s].astype(jnp.float32)
        att = (num / den).T
        att = jnp.concatenate([att[g * rows:(g + 1) * rows, :] for g in range(G)], axis=1)
        abuf[k, me_b * R + me_r] = att.astype(jnp.bfloat16)

        @pl.when(me_b < B - 1)
        def _():
            a_line(k, me_b, 0).start()

        @pl.when(me_b > 0)
        def _():
            a_line(k, me_b, 1).start()

        for d in range(1, R):
            a_core(k, me_b, d).start()

    def a_hop(k, h):
        @pl.when(me_b >= h)
        def _():
            o = me_b - h
            a_line(k, o, 0).wait_recv()

            @pl.when(me_b < B - 1)
            def _():
                a_line(k, o, 0).start()

            for d in range(1, R):
                a_core(k, o, d).start()

        @pl.when(me_b + h < B)
        def _():
            o = me_b + h
            a_line(k, o, 1).wait_recv()

            @pl.when(me_b > 0)
            def _():
                a_line(k, o, 1).start()

            for d in range(1, R):
                a_core(k, o, d).start()

    def a_drain():
        for k in range(K):
            for o in range(B):
                for d in range(1, R):
                    a_core(k, o, d).wait_send()

            @pl.when(me_b < B - 1)
            def _():
                for o in range(B):
                    @pl.when(me_b >= o)
                    def _():
                        a_line(k, o, 0).wait_send()

            @pl.when(me_b > 0)
            def _():
                for o in range(B):
                    @pl.when(me_b <= o)
                    def _():
                        a_line(k, o, 1).wait_send()

    def h_move(n, d):
        return remote(hsend.at[d - 1, n], hrecv.at[d - 1, n], h_ss.at[d - 1, n], h_rs.at[d - 1, n],
                      {"head": lax.rem(me_h + d, H)})

    def project(k):
        wcopies[k].wait()
        for o in range(B):
            for d in range(1, R):
                a_core_in(k, o, d).wait_recv()
        rowsk = jnp.concatenate([abuf[k, i].astype(jnp.float32) for i in range(B * R)], axis=0).astype(jnp.bfloat16)
        for n in range(nc):
            w = wv[k * feat:(k + 1) * feat, n * cw:(n + 1) * cw]
            y = jnp.dot(rowsk, w, preferred_element_type=jnp.float32)
            if k > 0:
                y = y + acc[n]
            acc[n] = y
            if k == K - 1:
                for d in range(1, H):
                    to = lax.rem(me_h + d, H)
                    hsend[d - 1, n] = acc[n, pl.ds(pl.multiple_of(to * share, share), share), :].astype(jnp.bfloat16)
                    h_move(n, d).start()

    near = jnp.where(p < S // 2, 0, 1)

    def line_move(w, k, o, acc_src, stat_src):
        to = holder(p + 1 - 2 * w)
        return (
            remote(acc_src, lin.at[w, k, o], l_ss.at[w, k, o], l_rs.at[w, k, o], to),
            remote(stat_src, lstat.at[w, k, o], s_ss.at[w, k, o], s_rs.at[w, k, o], to),
        )

    def line_source(k, o):
        @pl.when(p == 0)
        def _():
            for c in line_move(0, k, o, pbuf.at[k, o], pstat.at[k, o]):
                c.start()

        @pl.when(p == S - 1)
        def _():
            for c in line_move(1, k, o, pbuf.at[k, o], pstat.at[k, o]):
                c.start()

    def line_step(w, k, o):
        @pl.when((p > 0) & (p < S - 1))
        def _():
            for c in line_move(w, k, o, lout.at[w, k, o], lostat.at[w, k, o]):
                c.wait_recv()
            m_in, m_own = lstat[w, k, o, 0:1], pstat[k, o, 0:1]
            top = jnp.maximum(m_in, m_own)
            f_in, f_own = jnp.exp2((m_in - top) * scale2), jnp.exp2((m_own - top) * scale2)
            lout[w, k, o] = (
                f_in * lin[w, k, o].astype(jnp.float32) + f_own * pbuf[k, o].astype(jnp.float32)
            ).astype(jnp.bfloat16)
            lostat[w, k, o, 0:1] = top
            lostat[w, k, o, 1:2] = f_in * lstat[w, k, o, 1:2] + f_own * pstat[k, o, 1:2]
            for c in line_move(w, k, o, lout.at[w, k, o], lostat.at[w, k, o]):
                c.start()

    def line_final(k, o):
        @pl.when(p == 0)
        def _():
            for c in line_move(1, k, o, lout.at[1, k, o], lostat.at[1, k, o]):
                c.wait_recv()

        @pl.when(p == S - 1)
        def _():
            for c in line_move(0, k, o, lout.at[0, k, o], lostat.at[0, k, o]):
                c.wait_recv()

        stats = [pstat[k, o], lstat[0, k, o], lstat[1, k, o]]
        accs = [pbuf[k, o], lin[0, k, o], lin[1, k, o]]
        top = functools.reduce(jnp.maximum, [x[0:1] for x in stats])
        den = jnp.zeros((1, group), jnp.float32)
        num = jnp.zeros((HD, group), jnp.float32)
        for x, y in zip(stats, accs):
            f = jnp.exp2((x[0:1] - top) * scale2)
            den = den + f * x[1:2]
            num = num + f * y.astype(jnp.float32)
        att = (num / den).T
        att = jnp.concatenate([att[g * rows:(g + 1) * rows, :] for g in range(G)], axis=1)
        abuf[k, o * R + me_r] = att.astype(jnp.bfloat16)
        for d in range(1, R):
            a_core(k, o, d).start()

    def line_drain():
        for k in range(K):
            for o in range(S):
                for w in range(2):
                    @pl.when(p != (S - 1) * (1 - w))
                    def _():
                        for c in line_move(w, k, o, pbuf.at[k, o], pstat.at[k, o]):
                            c.wait_send()
                for d in range(1, R):
                    a_core(k, o, d).wait_send()

    early = max(1, K - 1)
    for k in range(early):
        q_start(k)
    if stride == 1:
        for w in range(2):
            @pl.when(p == (S - 1) * w)
            def _():
                for k in range(K):
                    for o in range(S):
                        lin[w, k, o] = jnp.zeros((HD, group), jnp.bfloat16)
                        lstat[w, k, o, 0:1] = jnp.full((1, group), NEG, jnp.float32)
                        lstat[w, k, o, 1:2] = jnp.zeros((1, group), jnp.float32)
    kcopy.wait()
    vcopy.wait()
    lax.fori_loop(0, slab // step, split, 0)
    if S > 1 and K > early:
        _, h, j = hops.pop(0)
        q_hop(j, h)
    for k in range(early, K):
        q_start(k)
    if stride == 1:
        for t in range(K + 4):
            if t < K:
                q_ready(t)
                wcopies[t].start()
                attend(t)
                for o in range(S):
                    line_source(t, o)
            for o in range(S):
                if 0 <= t - 1 < K:
                    line_step(near, t - 1, o)
                if 0 <= t - 2 < K:
                    line_step(1 - near, t - 2, o)
            if 0 <= t - 3 < K:
                for o in range(S):
                    line_final(t - 3, o)
            if 0 <= t - 4 < K:
                project(t - 4)
    else:
        for k in range(K):
            q_ready(k)
            wcopies[k].start()
            attend(k)
            p_send(k)
        for k in range(K):
            combine(k)
        for k in range(K):
            for h in range(1, B):
                a_hop(k, h)
            project(k)
    own = pl.ds(pl.multiple_of(me_h * share, share), share)
    for n in range(nc):
        y = acc[n, own, :]
        for d in range(1, H):
            h_move(n, d).wait_recv()
            y = y + hrecv[d - 1, n].astype(jnp.float32)
        out[:, n * cw:(n + 1) * cw] = y.astype(jnp.bfloat16)
    q_drain()
    if stride == 1:
        line_drain()
    else:
        for k in range(K):
            for d in range(1, S):
                for c in p_move(k, lax.rem(p + d, S), p):
                    c.wait_send()
        a_drain()
    for n in range(nc):
        for d in range(1, H):
            h_move(n, d).wait_send()


def body(query, keys, values, lengths, out_weight):
    rows = query.shape[0]
    slab, K, HD = keys.shape[2:]
    B = lax.axis_size("blk")
    R = lax.axis_size("rep")
    H = lax.axis_size("head")
    S = min(8, B)
    stride = B // S
    G = query.shape[1] // (K * HD)
    feat = G * HD
    group = G * rows
    lanes = S * group
    depth, cols = out_weight.shape
    total = B * R * rows
    share = total // H
    nc = max(1, cols // 512)
    cw = cols // nc
    line = (2, K, S) if stride == 1 else (1, 1, 1)
    dims = (B, R, H, S, stride, rows, K, G, HD, slab)
    bf, f32 = jnp.bfloat16, jnp.float32
    vm, dma = pltpu.VMEM, pltpu.SemaphoreType.DMA
    any_spec = pl.BlockSpec(memory_space=pltpu.HBM)
    return pl.pallas_call(
        functools.partial(kernel, dims),
        out_shape=jax.ShapeDtypeStruct((share, cols), bf),
        in_specs=[
            pl.BlockSpec(memory_space=pltpu.SMEM),
            pl.BlockSpec(memory_space=pltpu.VMEM),
            any_spec, any_spec, any_spec,
        ],
        out_specs=pl.BlockSpec(memory_space=pltpu.VMEM),
        scratch_shapes=[
            vm((depth, cols), bf),
            vm((slab * K, HD), bf),
            vm((slab * K, HD), bf),
            vm((K, slab, HD), bf),
            vm((K, HD, slab), bf),
            vm((2, 256 * K, HD), f32),
            vm((slab, lanes), f32),
            vm((slab, lanes), bf),
            vm((K, S, rows, feat), bf),
            vm((lanes, HD), bf),
            vm((K, S, HD, group), bf),
            vm((K, S, 2, group), f32),
            vm((K, S, HD, group), bf),
            vm((K, S, 2, group), f32),
            vm((K, B * R, rows, feat), bf),
            vm((nc, total, cw), f32),
            vm((max(1, H - 1), nc, share, cw), bf),
            vm((max(1, H - 1), nc, share, cw), bf),
            vm(line + (HD, group), bf),
            vm(line + (2, group), f32),
            vm(line + (HD, group), bf),
            vm(line + (2, group), f32),
            dma((K,)),
            dma((2,)),
            dma((K, S, 2)), dma((K, S)),
            dma((K, S)), dma((K, S)),
            dma((K, S)), dma((K, S)),
            dma((K, B, 2)), dma((K, B)),
            dma((K, B, max(1, R - 1))), dma((K, B, max(1, R - 1))),
            dma((max(1, H - 1), nc)), dma((max(1, H - 1), nc)),
            dma(line), dma(line), dma(line), dma(line),
        ],
        compiler_params=pltpu.CompilerParams(
            collective_id=0, has_side_effects=True, vmem_limit_bytes=61 * 1024 * 1024),
        name="attend_project",
    )(lengths, query, keys.reshape(slab * K, HD), values.reshape(slab * K, HD), out_weight)


def solution(mesh):
    return jax.shard_map(
        body,
        mesh=mesh,
        in_specs=(
            P(("groups", "blk", "rep"), "head"),
            P(("groups", "blk"), "rep", None, "head", None),
            P(("groups", "blk"), "rep", None, "head", None),
            P("groups"),
            P("head", ("blk", "rep")),
        ),
        out_specs=P(("groups", "head"), ("blk", "rep")),
        check_vma=False,
    )
```

```python
import functools
import jax
import jax.numpy as jnp
from jax import lax
from jax.experimental import pallas as pl
from jax.experimental.pallas import tpu as pltpu
from jax.sharding import PartitionSpec as P

NEG = -1e30
LOG2E = 1.4426950408889634
MESH = pl.DeviceIdType.MESH


def remote(src, dst, ssem, rsem, where):
    return pltpu.make_async_remote_copy(
        src_ref=src, dst_ref=dst, send_sem=ssem, recv_sem=rsem,
        device_id=where, device_id_type=MESH)


def kernel(
    dims, lengths, query, keys, values, weight, out,
    wv, kraw, vraw, kh, vt, fbuf, sbuf, wbuf, qbuf, qmat, pbuf, pstat, rbuf, rstat,
    abuf, acc, hsend, hrecv, lin, lstat, lout, lostat,
    wsem, ksem, q_ss, q_rs, p_ss, p_rs, t_ss, t_rs, a_ss, a_rs, c_ss, c_rs, h_ss, h_rs,
    l_ss, l_rs, s_ss, s_rs,
):
    B, R, H, S, stride, rows, K, G, HD, slab = dims
    heads = pl.ds
    group = G * rows
    lanes = S * group
    feat = G * HD
    cols = weight.shape[1]
    total = B * R * rows
    share = total // H
    nc = hsend.shape[1]
    cw = cols // nc
    scale2 = (HD ** -0.5) * LOG2E
    me_b = lax.axis_index("blk")
    me_r = lax.axis_index("rep")
    me_h = lax.axis_index("head")
    p = me_b // stride
    base = lax.rem(me_b, stride)

    def holder(q):
        return {"blk": q * stride + base}

    kcopy = pltpu.make_async_copy(keys, kraw, ksem.at[0])
    vcopy = pltpu.make_async_copy(values, vraw, ksem.at[1])
    kcopy.start()
    vcopy.start()
    wcopies = [
        pltpu.make_async_copy(weight.at[pl.ds(k * feat, feat)], wv.at[pl.ds(k * feat, feat)], wsem.at[k])
        for k in range(K)
    ]

    barrier = pltpu.get_barrier_semaphore()
    for d in range(1, S):
        pl.semaphore_signal(barrier, inc=1, device_id=holder(lax.rem(p + d, S)), device_id_type=MESH)
    for d in range(1, R):
        pl.semaphore_signal(barrier, inc=1, device_id={"rep": lax.rem(me_r + d, R)}, device_id_type=MESH)
    for d in range(1, H):
        pl.semaphore_signal(barrier, inc=1, device_id={"head": lax.rem(me_h + d, H)}, device_id_type=MESH)
    if stride > 1:
        for d in (1, B - 1):
            pl.semaphore_signal(barrier, inc=1, device_id={"blk": lax.rem(me_b + d, B)}, device_id_type=MESH)
    pl.semaphore_wait(barrier, (S - 1) + (R - 1) + (H - 1) + (2 if stride > 1 else 0))

    def q_move(k, o, side, src):
        to = p + 1 if side == 0 else p - 1
        return remote(src, qbuf.at[k, o], q_ss.at[k, o, side], q_rs.at[k, o], holder(to))

    def own_q(k):
        return query.at[:, pl.ds(k * feat, feat)]

    def q_start(k):
        @pl.when(p < S - 1)
        def _():
            q_move(k, p, 0, own_q(k)).start()

        @pl.when(p > 0)
        def _():
            q_move(k, p, 1, own_q(k)).start()

        qbuf[k, p] = query[:, k * feat:(k + 1) * feat]

    def q_hop(k, h):
        @pl.when(p >= h)
        def _():
            o = p - h
            q_move(k, o, 0, qbuf.at[k, o]).wait_recv()

            @pl.when(p < S - 1)
            def _():
                q_move(k, o, 0, qbuf.at[k, o]).start()

        @pl.when(p + h < S)
        def _():
            o = p + h
            q_move(k, o, 1, qbuf.at[k, o]).wait_recv()

            @pl.when(p > 0)
            def _():
                q_move(k, o, 1, qbuf.at[k, o]).start()

    hops = sorted((k + 2 * h, h, k) for k in range(K) for h in range(1, S))

    def q_ready(k):
        while hops and hops[0][0] <= k + 2 * (S - 1):
            _, h, j = hops.pop(0)
            q_hop(j, h)

    def q_drain():
        for k in range(K):
            @pl.when(p < S - 1)
            def _():
                q_move(k, p, 0, own_q(k)).wait_send()
                for h in range(1, S):
                    @pl.when(p >= h)
                    def _():
                        q_move(k, p - h, 0, qbuf.at[k, p - h]).wait_send()

            @pl.when(p > 0)
            def _():
                q_move(k, p, 1, own_q(k)).wait_send()
                for h in range(1, S):
                    @pl.when(p + h < S)
                    def _():
                        q_move(k, p + h, 1, qbuf.at[k, p + h]).wait_send()

    sub = lax.rem(lax.broadcasted_iota(jnp.int32, (1, group), 1), rows)
    pieces = []
    for o in range(S):
        first = ((o * stride + base) * R + me_r) * rows
        piece = jnp.zeros((1, group), jnp.int32)
        for r in range(rows):
            piece = jnp.where(sub == r, lengths[first + r], piece)
        pieces.append(piece)
    live_to = jnp.concatenate(pieces, axis=1) - p * slab

    step = 256

    def split(c, carry):
        src = pl.ds(pl.multiple_of(c * step * K, step * K), step * K)
        dst = pl.ds(pl.multiple_of(c * step, step), step)
        fbuf[0] = kraw[src, :].astype(jnp.float32)
        fbuf[1] = vraw[src, :].astype(jnp.float32)
        for k in range(K):
            kh[k, dst, :] = fbuf[0, pl.ds(k, step, stride=K), :].astype(jnp.bfloat16)
            vt[k, :, dst] = fbuf[1, pl.ds(k, step, stride=K), :].T.astype(jnp.bfloat16)
        return carry

    def attend(k):
        for o in range(S):
            x = qbuf[k, o].astype(jnp.float32)
            x = jnp.concatenate([x[:, g * HD:(g + 1) * HD] for g in range(G)], axis=0)
            qmat[o * group:(o + 1) * group, :] = x.astype(jnp.bfloat16)
        qk = qmat[...]
        iota = lax.broadcasted_iota(jnp.int32, (step, lanes), 0)

        def first(c, m):
            at = pl.ds(pl.multiple_of(c * step, step), step)
            s = lax.dot_general(kh[k, at, :], qk, (((1,), (1,)), ((), ())), preferred_element_type=jnp.float32)
            s = jnp.where(iota < live_to - c * step, s, NEG)
            sbuf[at, :] = s
            return jnp.maximum(m, jnp.max(s.reshape(step // 8, 8, lanes), axis=0))

        m = lax.fori_loop(0, slab // step, first, jnp.full((8, lanes), NEG, jnp.float32), unroll=4)
        m = jnp.max(m, axis=0, keepdims=True)

        def second(c, l):
            at = pl.ds(pl.multiple_of(c * step, step), step)
            e = jnp.exp2((sbuf[at, :] - m) * scale2)
            wbuf[at, :] = e.astype(jnp.bfloat16)
            return l + jnp.sum(e.reshape(step // 8, 8, lanes), axis=0)

        l = lax.fori_loop(0, slab // step, second, jnp.zeros((8, lanes), jnp.float32), unroll=4)
        l = jnp.sum(l, axis=0, keepdims=True)
        part = jnp.dot(vt[k], wbuf[...], preferred_element_type=jnp.float32).astype(jnp.bfloat16)
        for o in range(S):
            at = slice(o * group, (o + 1) * group)
            pbuf[k, o] = part[:, at]
            pstat[k, o, 0:1] = m[:, at]
            pstat[k, o, 1:2] = l[:, at]

    def p_move(k, to, frm):
        return (
            remote(pbuf.at[k, to], rbuf.at[k, frm], p_ss.at[k, to], p_rs.at[k, frm], holder(to)),
            remote(pstat.at[k, to], rstat.at[k, frm], t_ss.at[k, to], t_rs.at[k, frm], holder(to)),
        )

    def p_send(k):
        for d in range(1, S):
            for c in p_move(k, lax.rem(p + d, S), p):
                c.start()
        rbuf[k, p] = pbuf[k, p]
        rstat[k, p] = pstat[k, p]

    def a_line(k, o, side):
        to = me_b + 1 if side == 0 else me_b - 1
        slot = abuf.at[k, o * R + me_r]
        return remote(slot, slot, a_ss.at[k, o, side], a_rs.at[k, o], {"blk": to})

    def a_core(k, o, d):
        slot = abuf.at[k, o * R + me_r]
        return remote(slot, slot, c_ss.at[k, o, d - 1], c_rs.at[k, o, d - 1], {"rep": lax.rem(me_r + d, R)})

    def a_core_in(k, o, d):
        slot = abuf.at[k, o * R + lax.rem(me_r + R - d, R)]
        return remote(slot, slot, c_ss.at[k, o, d - 1], c_rs.at[k, o, d - 1], {"rep": lax.rem(me_r + d, R)})

    def combine(k):
        for d in range(1, S):
            for c in p_move(k, lax.rem(p + d, S), lax.rem(p + S - d, S)):
                c.wait_recv()
        best = [rstat[k, s, 0:1] for s in range(S)]
        top = functools.reduce(jnp.maximum, best)
        den = jnp.zeros((1, group), jnp.float32)
        num = jnp.zeros((HD, group), jnp.float32)
        for s in range(S):
            f = jnp.exp2((best[s] - top) * scale2)
            den = den + f * rstat[k, s, 1:2]
            num = num + f * rbuf[k, s].astype(jnp.float32)
        att = (num / den).T
        att = jnp.concatenate([att[g * rows:(g + 1) * rows, :] for g in range(G)], axis=1)
        abuf[k, me_b * R + me_r] = att.astype(jnp.bfloat16)

        @pl.when(me_b < B - 1)
        def _():
            a_line(k, me_b, 0).start()

        @pl.when(me_b > 0)
        def _():
            a_line(k, me_b, 1).start()

        for d in range(1, R):
            a_core(k, me_b, d).start()

    def a_hop(k, h):
        @pl.when(me_b >= h)
        def _():
            o = me_b - h
            a_line(k, o, 0).wait_recv()

            @pl.when(me_b < B - 1)
            def _():
                a_line(k, o, 0).start()

            for d in range(1, R):
                a_core(k, o, d).start()

        @pl.when(me_b + h < B)
        def _():
            o = me_b + h
            a_line(k, o, 1).wait_recv()

            @pl.when(me_b > 0)
            def _():
                a_line(k, o, 1).start()

            for d in range(1, R):
                a_core(k, o, d).start()

    def a_drain():
        for k in range(K):
            for o in range(B):
                for d in range(1, R):
                    a_core(k, o, d).wait_send()

            @pl.when(me_b < B - 1)
            def _():
                for o in range(B):
                    @pl.when(me_b >= o)
                    def _():
                        a_line(k, o, 0).wait_send()

            @pl.when(me_b > 0)
            def _():
                for o in range(B):
                    @pl.when(me_b <= o)
                    def _():
                        a_line(k, o, 1).wait_send()

    def h_move(n, d):
        return remote(hsend.at[d - 1, n], hrecv.at[d - 1, n], h_ss.at[d - 1, n], h_rs.at[d - 1, n],
                      {"head": lax.rem(me_h + d, H)})

    def project(k):
        wcopies[k].wait()
        for o in range(B):
            for d in range(1, R):
                a_core_in(k, o, d).wait_recv()
        rowsk = jnp.concatenate([abuf[k, i].astype(jnp.float32) for i in range(B * R)], axis=0).astype(jnp.bfloat16)
        for n in range(nc):
            w = wv[k * feat:(k + 1) * feat, n * cw:(n + 1) * cw]
            y = jnp.dot(rowsk, w, preferred_element_type=jnp.float32)
            if k > 0:
                y = y + acc[n]
            acc[n] = y
            if k == K - 1:
                for d in range(1, H):
                    to = lax.rem(me_h + d, H)
                    hsend[d - 1, n] = acc[n, pl.ds(pl.multiple_of(to * share, share), share), :].astype(jnp.bfloat16)
                    h_move(n, d).start()

    near = jnp.where(p < S // 2, 0, 1)

    def line_move(w, k, o, acc_src, stat_src):
        to = holder(p + 1 - 2 * w)
        return (
            remote(acc_src, lin.at[w, k, o], l_ss.at[w, k, o], l_rs.at[w, k, o], to),
            remote(stat_src, lstat.at[w, k, o], s_ss.at[w, k, o], s_rs.at[w, k, o], to),
        )

    def line_source(k, o):
        @pl.when(p == 0)
        def _():
            for c in line_move(0, k, o, pbuf.at[k, o], pstat.at[k, o]):
                c.start()

        @pl.when(p == S - 1)
        def _():
            for c in line_move(1, k, o, pbuf.at[k, o], pstat.at[k, o]):
                c.start()

    def line_step(w, k, o):
        @pl.when((p > 0) & (p < S - 1))
        def _():
            for c in line_move(w, k, o, lout.at[w, k, o], lostat.at[w, k, o]):
                c.wait_recv()
            m_in, m_own = lstat[w, k, o, 0:1], pstat[k, o, 0:1]
            top = jnp.maximum(m_in, m_own)
            f_in, f_own = jnp.exp2((m_in - top) * scale2), jnp.exp2((m_own - top) * scale2)
            lout[w, k, o] = (
                f_in * lin[w, k, o].astype(jnp.float32) + f_own * pbuf[k, o].astype(jnp.float32)
            ).astype(jnp.bfloat16)
            lostat[w, k, o, 0:1] = top
            lostat[w, k, o, 1:2] = f_in * lstat[w, k, o, 1:2] + f_own * pstat[k, o, 1:2]
            for c in line_move(w, k, o, lout.at[w, k, o], lostat.at[w, k, o]):
                c.start()

    def line_final(k, o):
        @pl.when(p == 0)
        def _():
            for c in line_move(1, k, o, lout.at[1, k, o], lostat.at[1, k, o]):
                c.wait_recv()

        @pl.when(p == S - 1)
        def _():
            for c in line_move(0, k, o, lout.at[0, k, o], lostat.at[0, k, o]):
                c.wait_recv()

        stats = [pstat[k, o], lstat[0, k, o], lstat[1, k, o]]
        accs = [pbuf[k, o], lin[0, k, o], lin[1, k, o]]
        top = functools.reduce(jnp.maximum, [x[0:1] for x in stats])
        den = jnp.zeros((1, group), jnp.float32)
        num = jnp.zeros((HD, group), jnp.float32)
        for x, y in zip(stats, accs):
            f = jnp.exp2((x[0:1] - top) * scale2)
            den = den + f * x[1:2]
            num = num + f * y.astype(jnp.float32)
        att = (num / den).T
        att = jnp.concatenate([att[g * rows:(g + 1) * rows, :] for g in range(G)], axis=1)
        abuf[k, o * R + me_r] = att.astype(jnp.bfloat16)
        for d in range(1, R):
            a_core(k, o, d).start()

    def line_drain():
        for k in range(K):
            for o in range(S):
                for w in range(2):
                    @pl.when(p != (S - 1) * (1 - w))
                    def _():
                        for c in line_move(w, k, o, pbuf.at[k, o], pstat.at[k, o]):
                            c.wait_send()
                for d in range(1, R):
                    a_core(k, o, d).wait_send()

    early = max(1, K - 1)
    for k in range(early):
        q_start(k)
    if stride == 1:
        for w in range(2):
            @pl.when(p == (S - 1) * w)
            def _():
                for k in range(K):
                    for o in range(S):
                        lin[w, k, o] = jnp.zeros((HD, group), jnp.bfloat16)
                        lstat[w, k, o, 0:1] = jnp.full((1, group), NEG, jnp.float32)
                        lstat[w, k, o, 1:2] = jnp.zeros((1, group), jnp.float32)
    kcopy.wait()
    vcopy.wait()
    lax.fori_loop(0, slab // step, split, 0)
    if S > 1 and K > early:
        _, h, j = hops.pop(0)
        q_hop(j, h)
    for k in range(early, K):
        q_start(k)
    if stride == 1:
        for t in range(K + 4):
            if t < K:
                q_ready(t)
                attend(t)
                for o in range(S):
                    line_source(t, o)
            if 0 <= t - 1 < K:
                wcopies[t - 1].start()
            for o in range(S):
                if 0 <= t - 1 < K:
                    line_step(near, t - 1, o)
                if 0 <= t - 2 < K:
                    line_step(1 - near, t - 2, o)
            if 0 <= t - 3 < K:
                for o in range(S):
                    line_final(t - 3, o)
            if 0 <= t - 4 < K:
                project(t - 4)
    else:
        for k in range(K):
            q_ready(k)
            wcopies[k].start()
            attend(k)
            p_send(k)
        for k in range(K):
            combine(k)
        for k in range(K):
            for h in range(1, B):
                a_hop(k, h)
            project(k)
    own = pl.ds(pl.multiple_of(me_h * share, share), share)
    for n in range(nc):
        y = acc[n, own, :]
        for d in range(1, H):
            h_move(n, d).wait_recv()
            y = y + hrecv[d - 1, n].astype(jnp.float32)
        out[:, n * cw:(n + 1) * cw] = y.astype(jnp.bfloat16)
    q_drain()
    if stride == 1:
        line_drain()
    else:
        for k in range(K):
            for d in range(1, S):
                for c in p_move(k, lax.rem(p + d, S), p):
                    c.wait_send()
        a_drain()
    for n in range(nc):
        for d in range(1, H):
            h_move(n, d).wait_send()


def body(query, keys, values, lengths, out_weight):
    rows = query.shape[0]
    slab, K, HD = keys.shape[2:]
    B = lax.axis_size("blk")
    R = lax.axis_size("rep")
    H = lax.axis_size("head")
    S = min(8, B)
    stride = B // S
    G = query.shape[1] // (K * HD)
    feat = G * HD
    group = G * rows
    lanes = S * group
    depth, cols = out_weight.shape
    total = B * R * rows
    share = total // H
    nc = max(1, cols // 512)
    cw = cols // nc
    line = (2, K, S) if stride == 1 else (1, 1, 1)
    dims = (B, R, H, S, stride, rows, K, G, HD, slab)
    bf, f32 = jnp.bfloat16, jnp.float32
    vm, dma = pltpu.VMEM, pltpu.SemaphoreType.DMA
    any_spec = pl.BlockSpec(memory_space=pltpu.HBM)
    return pl.pallas_call(
        functools.partial(kernel, dims),
        out_shape=jax.ShapeDtypeStruct((share, cols), bf),
        in_specs=[
            pl.BlockSpec(memory_space=pltpu.SMEM),
            pl.BlockSpec(memory_space=pltpu.VMEM),
            any_spec, any_spec, any_spec,
        ],
        out_specs=pl.BlockSpec(memory_space=pltpu.VMEM),
        scratch_shapes=[
            vm((depth, cols), bf),
            vm((slab * K, HD), bf),
            vm((slab * K, HD), bf),
            vm((K, slab, HD), bf),
            vm((K, HD, slab), bf),
            vm((2, 256 * K, HD), f32),
            vm((slab, lanes), f32),
            vm((slab, lanes), bf),
            vm((K, S, rows, feat), bf),
            vm((lanes, HD), bf),
            vm((K, S, HD, group), bf),
            vm((K, S, 2, group), f32),
            vm((K, S, HD, group), bf),
            vm((K, S, 2, group), f32),
            vm((K, B * R, rows, feat), bf),
            vm((nc, total, cw), f32),
            vm((max(1, H - 1), nc, share, cw), bf),
            vm((max(1, H - 1), nc, share, cw), bf),
            vm(line + (HD, group), bf),
            vm(line + (2, group), f32),
            vm(line + (HD, group), bf),
            vm(line + (2, group), f32),
            dma((K,)),
            dma((2,)),
            dma((K, S, 2)), dma((K, S)),
            dma((K, S)), dma((K, S)),
            dma((K, S)), dma((K, S)),
            dma((K, B, 2)), dma((K, B)),
            dma((K, B, max(1, R - 1))), dma((K, B, max(1, R - 1))),
            dma((max(1, H - 1), nc)), dma((max(1, H - 1), nc)),
            dma(line), dma(line), dma(line), dma(line),
        ],
        compiler_params=pltpu.CompilerParams(
            collective_id=0, has_side_effects=True, vmem_limit_bytes=61 * 1024 * 1024),
        name="attend_project",
    )(lengths, query, keys.reshape(slab * K, HD), values.reshape(slab * K, HD), out_weight)


def solution(mesh):
    return jax.shard_map(
        body,
        mesh=mesh,
        in_specs=(
            P(("groups", "blk", "rep"), "head"),
            P(("groups", "blk"), "rep", None, "head", None),
            P(("groups", "blk"), "rep", None, "head", None),
            P("groups"),
            P("head", ("blk", "rep")),
        ),
        out_specs=P(("groups", "head"), ("blk", "rep")),
        check_vma=False,
    )
```
